32 devices in a mesh: pair: 8 (over z, core), cd: 4 (over y, x).
Axes of the slice: x: 2, y: 2, z: 4, core: 2. Of those that a mesh axis runs over, the one named last changes fastest.
Arguments:
- amplitudes: float32 [2048, 4096], P('pair', 'cd'), may hold values from -6 to 6
- integrals: float32 [4096, 256], P(('cd', 'pair')), may hold values from -0.09375 to 0.09375
- keep_tiles: int32 [32, 2], replicated, may hold values from 0 to 1, as said below
Outputs:
- ladder: float32 [2048, 256], P(('pair', 'cd'))
The draws below stay inside these ranges and needn't reach their ends.
Inputs may be any that keep to these rules, and one draw needn't show every extreme that they name: `keep_tiles`: each entry is 0 (tile screened out) or 1 (tile kept); each tile row keeps at most one tile, and some tile row keeps one.
All inputs are finite; a program needn't handle non-finite values.
Results may differ from the reference program's by a relative error of at most 0.000071.
Values sent between devices are 32-bit elements; how exact they have to be, the bound alone decides.
A program may use at most 64 MiB of HBM per device.

```python
import jax
import jax.numpy as jnp
from jax import lax

TILE = 128
AB = 256
CD = 4096
PAIRS = 2048


def draw_keep_tiles(key, part):
    rows_total = CD // TILE
    blocks = AB // TILE
    key_col = jax.random.fold_in(key, 11)
    key_live = jax.random.fold_in(key, 23)
    column = jax.random.randint(key_col, (rows_total,), 0, blocks)
    live = (jax.random.randint(key_live, (rows_total,), 0, 10) < 9).astype(jnp.int32)
    live = jnp.where(jnp.arange(rows_total) == 0, 1, live)
    onehot = (column[:, None] == jnp.arange(blocks)[None, :]).astype(jnp.int32)
    return onehot * live[:, None]


def block_levels(own_key, extent, pieces, low, high):
    def one(axis_at, shards_of):
        draws = jax.random.uniform(jax.random.fold_in(jax.random.fold_in(own_key, 6), axis_at), (shards_of,), jnp.float32, low / len(pieces), high / len(pieces))
        return jnp.repeat(jnp.exp(draws), extent[axis_at] // shards_of).reshape((-1,) + (1,) * (len(extent) - axis_at - 1))

    loudness = one(*pieces[0])
    for cut in pieces[1:]:
        loudness = loudness * one(*cut)
    return loudness


def noise(rng, extent, scale, most, pieces=(), dtype=jnp.bfloat16):
    gain = block_levels(rng, extent, pieces, -0.22, 0.18) if pieces else 1.0
    drawn = jax.random.normal(rng, extent, jnp.float32) * scale * gain
    return jnp.minimum(jnp.maximum(drawn, -most), most).astype(dtype)


def setup_inputs(seed: int = 0) -> dict:
    keys = jax.random.split(jax.random.key(seed), 4)
    amplitudes = noise(keys[0], (PAIRS, CD), 1.0, 6.0, ((0, 8), (1, 4)), jnp.float32)
    integrals = noise(keys[1], (CD, AB), CD ** -0.5, 0.09375, ((0, 32),), jnp.float32)
    keep_tiles = draw_keep_tiles(jax.random.fold_in(keys[3], 71), 0)
    return {"amplitudes": amplitudes, "integrals": integrals, "keep_tiles": keep_tiles}


def reference(amplitudes, integrals, keep_tiles):
    flags = keep_tiles.astype(jnp.float32)
    flags = jnp.repeat(jnp.repeat(flags, TILE, axis=0), TILE, axis=1)
    screened = integrals * flags
    return jnp.dot(amplitudes, screened, precision=lax.Precision.HIGHEST, preferred_element_type=jnp.float32)
```

```python
import functools

import jax
import jax.numpy as jnp
from jax import lax
from jax.experimental import pallas as pl
from jax.experimental.pallas import tpu as pltpu
from jax.sharding import PartitionSpec as P

TILE = 128
CORES = 2
CHUNKS = 2
MESH = pl.DeviceIdType.MESH


def flip(i, bits):
    b = 1
    out = i
    while b <= bits:
        if bits & b:
            out = out + b - 2 * b * (lax.rem(lax.div(i, b), 2))
        b *= 2
    return out


def split(x):
    hi = x.astype(jnp.bfloat16)
    lo = (x - hi.astype(jnp.float32)).astype(jnp.bfloat16)
    return hi, lo


def dot3(a_hi, a_lo, b_hi, b_lo):
    d = functools.partial(jnp.dot, preferred_element_type=jnp.float32)
    return d(a_hi, b_hi) + (d(a_lo, b_hi) + d(a_hi, b_lo))


def kernel(pairs, cds, flags, v_hbm, a_hbm, out_ref, v, a, tiles, a_hi, a_lo, acc, land,
           load_sem, ssem, rsem, psend, precv, rs_send, rs_recv):
    nz = pairs // CORES
    me = lax.axis_index("pair")
    cd = lax.axis_index("cd")
    z = lax.div(me, CORES)
    core = lax.rem(me, CORES)
    partner = me + 1 - 2 * core
    blocks = v.shape[1] // TILE
    part = TILE // CHUNKS
    rows = out_ref.shape[0]

    load_v = pltpu.make_async_copy(v_hbm, v, load_sem.at[0])
    load_v.start()
    load_a = pltpu.make_async_copy(a_hbm, a, load_sem.at[1])
    load_a.start()

    has_next = (z + 1 < nz, z > 0)
    neighbour = (me + CORES, me - CORES)

    barrier = pltpu.get_barrier_semaphore()
    for d in range(2):
        @pl.when(has_next[d])
        def _():
            pl.semaphore_signal(barrier, inc=1, device_id={"pair": neighbour[d]}, device_id_type=MESH)
    pl.semaphore_signal(barrier, inc=1, device_id={"pair": partner}, device_id_type=MESH)
    for j in range(1, cds):
        pl.semaphore_signal(barrier, inc=1, device_id={"cd": flip(cd, j)}, device_id_type=MESH)

    load_v.wait()
    row_block = cd * pairs + me
    own = v[:, :TILE] * flags[row_block, 0].astype(jnp.float32)
    for m in range(1, blocks):
        own = own + v[:, m * TILE:(m + 1) * TILE] * flags[row_block, m].astype(jnp.float32)
    tiles[me] = own

    greeted = cds + jnp.minimum(z, 1) + jnp.minimum(nz - 1 - z, 1)
    pl.semaphore_wait(barrier, greeted)

    def stream(d, s, c, k):
        r = pl.ds(c * part, part)
        return pltpu.make_async_remote_copy(
            src_ref=tiles.at[k, r], dst_ref=tiles.at[k, r],
            send_sem=ssem.at[d, s, c], recv_sem=rsem.at[d, s, c],
            device_id={"pair": neighbour[d]}, device_id_type=MESH)

    def exchange(d, s, c, k):
        r = pl.ds(c * part, part)
        return pltpu.make_async_remote_copy(
            src_ref=tiles.at[k, r], dst_ref=tiles.at[k, r],
            send_sem=psend.at[d, s, c], recv_sem=precv.at[d, s, c],
            device_id={"pair": partner}, device_id_type=MESH)

    def origin(d, s):
        return z - s if d == 0 else z + s

    def valid(d, s):
        return z - s >= 0 if d == 0 else z + s < nz

    for c in range(CHUNKS):
        for d in range(2):
            @pl.when(has_next[d])
            def _():
                stream(d, 0, c, me).start()
    for c in range(CHUNKS):
        exchange(0, 0, c, me).start()

    load_a.wait()
    hi, lo = split(a[...])
    a_hi[...] = hi
    a_lo[...] = lo

    def compute(d, s):
        chip = origin(d, s)
        for c in range(CHUNKS):
            exchange(d, s, c, chip * CORES + 1 - core).wait_recv()
        halves = []
        for i in range(CORES):
            k = chip * CORES + i
            t = tiles[k]
            g = cd * pairs + k
            halves.append(jnp.concatenate(
                [t * flags[g, m].astype(jnp.float32) for m in range(blocks)], axis=1))
        b_hi, b_lo = split(jnp.concatenate(halves, axis=0))
        cols = pl.ds(pl.multiple_of(chip * (CORES * TILE), CORES * TILE), CORES * TILE)
        prod = dot3(a_hi[:, cols], a_lo[:, cols], b_hi, b_lo)
        if s == 0:
            acc[...] = prod
        else:
            acc[...] += prod

    for s in range(1, nz):
        for c in range(CHUNKS):
            for d in range(2):
                @pl.when(valid(d, s))
                def _():
                    k = origin(d, s) * CORES + core
                    stream(d, s - 1, c, k).wait_recv()
                    if s < nz - 1:
                        @pl.when(has_next[d])
                        def _():
                            stream(d, s, c, k).start()
                    exchange(d, s, c, k).start()
        if s == 1:
            compute(0, 0)
        else:
            for d in range(2):
                @pl.when(valid(d, s - 1))
                def _():
                    compute(d, s - 1)
    for d in range(2):
        @pl.when(valid(d, nz - 1))
        def _():
            compute(d, nz - 1)

    def scatter(j):
        q = flip(cd, j)
        return pltpu.make_async_remote_copy(
            src_ref=acc.at[pl.ds(pl.multiple_of(q * rows, rows), rows)], dst_ref=land.at[j - 1],
            send_sem=rs_send.at[j - 1], recv_sem=rs_recv.at[j - 1],
            device_id={"cd": q}, device_id_type=MESH)

    for j in range(cds - 1, 0, -1):
        scatter(j).start()

    for c in range(CHUNKS):
        exchange(0, 0, c, me).wait_send()
        for d in range(2):
            @pl.when(has_next[d])
            def _():
                stream(d, 0, c, me).wait_send()
    for s in range(1, nz):
        for d in range(2):
            @pl.when(valid(d, s))
            def _():
                k = origin(d, s) * CORES + core
                for c in range(CHUNKS):
                    exchange(d, s, c, k).wait_send()
                if s < nz - 1:
                    @pl.when(has_next[d])
                    def _():
                        for c in range(CHUNKS):
                            stream(d, s, c, k).wait_send()

    total = acc[pl.ds(pl.multiple_of(cd * rows, rows), rows)]
    for j in range(1, cds):
        scatter(j).wait_recv()
        total = total + land[j - 1]
    out_ref[...] = total
    for j in range(1, cds):
        scatter(j).wait_send()


def solution(mesh):
    pairs, cds = mesh.shape["pair"], mesh.shape["cd"]
    nz = pairs // CORES

    def local(amplitudes, integrals, keep_tiles):
        n, depth = amplitudes.shape
        ab = integrals.shape[1]
        rows = n // cds
        return pl.pallas_call(
            functools.partial(kernel, pairs, cds),
            out_shape=jax.ShapeDtypeStruct((rows, ab), jnp.float32),
            in_specs=[
                pl.BlockSpec(memory_space=pltpu.SMEM),
                pl.BlockSpec(memory_space=pl.ANY),
                pl.BlockSpec(memory_space=pl.ANY),
            ],
            out_specs=pl.BlockSpec(memory_space=pltpu.VMEM),
            scratch_shapes=[
                pltpu.VMEM(integrals.shape, jnp.float32),
                pltpu.VMEM((n, depth), jnp.float32),
                pltpu.VMEM((pairs, TILE, TILE), jnp.float32),
                pltpu.VMEM((n, depth), jnp.bfloat16),
                pltpu.VMEM((n, depth), jnp.bfloat16),
                pltpu.VMEM((n, ab), jnp.float32),
                pltpu.VMEM((cds - 1, rows, ab), jnp.float32),
                pltpu.SemaphoreType.DMA((2,)),
                pltpu.SemaphoreType.DMA((2, nz, CHUNKS)),
                pltpu.SemaphoreType.DMA((2, nz, CHUNKS)),
                pltpu.SemaphoreType.DMA((2, nz, CHUNKS)),
                pltpu.SemaphoreType.DMA((2, nz, CHUNKS)),
                pltpu.SemaphoreType.DMA((cds - 1,)),
                pltpu.SemaphoreType.DMA((cds - 1,)),
            ],
            compiler_params=pltpu.CompilerParams(collective_id=0, has_side_effects=True),
        )(keep_tiles, integrals, amplitudes)

    placed = (P("pair", "cd"), P(("cd", "pair"), None), P())
    return jax.shard_map(
        local, mesh=mesh, in_specs=placed, out_specs=P(("pair", "cd"), None), check_vma=False
    )
```

```python
import functools

import jax
import jax.numpy as jnp
from jax import lax
from jax.experimental import pallas as pl
from jax.experimental.pallas import tpu as pltpu
from jax.sharding import PartitionSpec as P

TILE = 128
CORES = 2
CHUNKS = 2
MESH = pl.DeviceIdType.MESH


def flip(i, bits):
    b = 1
    out = i
    while b <= bits:
        if bits & b:
            out = out + b - 2 * b * (lax.rem(lax.div(i, b), 2))
        b *= 2
    return out


def split(x):
    hi = x.astype(jnp.bfloat16)
    lo = (x - hi.astype(jnp.float32)).astype(jnp.bfloat16)
    return hi, lo


def dot3(a_hi, a_lo, b_hi, b_lo):
    d = functools.partial(
        lax.dot_general, dimension_numbers=(((1,), (1,)), ((), ())), preferred_element_type=jnp.float32)
    return d(a_hi, b_hi) + (d(a_lo, b_hi) + d(a_hi, b_lo))


def kernel(pairs, cds, flags_hbm, v_hbm, a_hbm, out_ref, flags, v, a, tiles, a_hi, a_lo, acc, land,
           load_sem, ssem, rsem, psend, precv, rs_send, rs_recv):
    nz = pairs // CORES
    me = lax.axis_index("pair")
    cd = lax.axis_index("cd")
    z = lax.div(me, CORES)
    core = lax.rem(me, CORES)
    partner = me + 1 - 2 * core
    blocks = v.shape[1] // TILE
    part = TILE // CHUNKS
    rows = out_ref.shape[0]

    load_v = pltpu.make_async_copy(v_hbm, v, load_sem.at[0])
    load_v.start()
    load_f = pltpu.make_async_copy(flags_hbm, flags, load_sem.at[2])
    load_f.start()
    load_a = pltpu.make_async_copy(a_hbm, a, load_sem.at[1])
    load_a.start()

    has_next = (z + 1 < nz, z > 0)
    neighbour = (me + CORES, me - CORES)

    barrier = pltpu.get_barrier_semaphore()
    for d in range(2):
        @pl.when(has_next[d])
        def _():
            pl.semaphore_signal(barrier, inc=1, device_id={"pair": neighbour[d]}, device_id_type=MESH)
    for j in range(1, cds):
        pl.semaphore_signal(barrier, inc=1, device_id={"cd": flip(cd, j)}, device_id_type=MESH)
    pl.semaphore_signal(barrier, inc=1, device_id={"pair": partner}, device_id_type=MESH)

    load_f.wait()
    load_v.wait()
    row_block = cd * pairs + me
    own = v[:, :TILE] * flags[0, row_block].astype(jnp.float32)
    for m in range(1, blocks):
        own = own + v[:, m * TILE:(m + 1) * TILE] * flags[m, row_block].astype(jnp.float32)
    tiles[me] = own.T

    greeted = cds + jnp.minimum(z, 1) + jnp.minimum(nz - 1 - z, 1)
    pl.semaphore_wait(barrier, greeted)

    def stream(d, s, c, k):
        r = pl.ds(c * part, part)
        return pltpu.make_async_remote_copy(
            src_ref=tiles.at[k, r], dst_ref=tiles.at[k, r],
            send_sem=ssem.at[d, s, c], recv_sem=rsem.at[d, s, c],
            device_id={"pair": neighbour[d]}, device_id_type=MESH)

    def exchange(d, s, c, k):
        r = pl.ds(c * part, part)
        return pltpu.make_async_remote_copy(
            src_ref=tiles.at[k, r], dst_ref=tiles.at[k, r],
            send_sem=psend.at[d, s, c], recv_sem=precv.at[d, s, c],
            device_id={"pair": partner}, device_id_type=MESH)

    def origin(d, s):
        return z - s if d == 0 else z + s

    def valid(d, s):
        return z - s >= 0 if d == 0 else z + s < nz

    for c in range(CHUNKS):
        for d in (1, 0):
            @pl.when(has_next[d])
            def _():
                stream(d, 0, c, me).start()
    for c in range(CHUNKS):
        exchange(0, 0, c, me).start()

    load_a.wait()
    hi, lo = split(a[...])
    a_hi[...] = hi
    a_lo[...] = lo

    def compute(d, s, c):
        chip = origin(d, s)
        exchange(d, s, c, chip * CORES + 1 - core).wait_recv()
        halves = []
        for i in range(CORES):
            k = chip * CORES + i
            t = tiles[k, c * part:(c + 1) * part]
            g = cd * pairs + k
            halves.append(jnp.concatenate(
                [t * flags[m, g].astype(jnp.float32) for m in range(blocks)], axis=0))
        b_hi, b_lo = split(jnp.concatenate(halves, axis=1))
        cols = pl.ds(pl.multiple_of(chip * (CORES * TILE), CORES * TILE), CORES * TILE)
        prod = dot3(a_hi[:, cols], a_lo[:, cols], b_hi, b_lo)
        if s == 0:
            acc[c] = prod
        else:
            acc[c] += prod

    def compute_step(s, c):
        if s == 0:
            compute(0, 0, c)
        else:
            for d in range(2):
                @pl.when(valid(d, s))
                def _():
                    compute(d, s, c)

    for s in range(1, nz):
        for c in range(CHUNKS):
            for d in range(2):
                @pl.when(valid(d, s))
                def _():
                    k = origin(d, s) * CORES + core
                    stream(d, s - 1, c, k).wait_recv()
                    if s < nz - 1:
                        @pl.when(has_next[d])
                        def _():
                            stream(d, s, c, k).start()
                    exchange(d, s, c, k).start()
            compute_step(s - 1, c)

    def scatter(j, c):
        q = flip(cd, j)
        return pltpu.make_async_remote_copy(
            src_ref=acc.at[c, pl.ds(pl.multiple_of(q * rows, rows), rows)], dst_ref=land.at[j - 1, c],
            send_sem=rs_send.at[j - 1, c], recv_sem=rs_recv.at[j - 1, c],
            device_id={"cd": q}, device_id_type=MESH)

    for c in range(CHUNKS):
        compute_step(nz - 1, c)
        for j in range(cds - 1, 0, -1):
            scatter(j, c).start()

    for c in range(CHUNKS):
        exchange(0, 0, c, me).wait_send()
        for d in range(2):
            @pl.when(has_next[d])
            def _():
                stream(d, 0, c, me).wait_send()
    for s in range(1, nz):
        for d in range(2):
            @pl.when(valid(d, s))
            def _():
                k = origin(d, s) * CORES + core
                for c in range(CHUNKS):
                    exchange(d, s, c, k).wait_send()
                if s < nz - 1:
                    @pl.when(has_next[d])
                    def _():
                        for c in range(CHUNKS):
                            stream(d, s, c, k).wait_send()

    totals = []
    for c in range(CHUNKS):
        total = acc[c, pl.ds(pl.multiple_of(cd * rows, rows), rows)]
        for j in range(1, cds):
            scatter(j, c).wait_recv()
            total = total + land[j - 1, c]
        totals.append(total)
    for m in range(blocks):
        out_ref[:, m * TILE:(m + 1) * TILE] = jnp.concatenate(
            [t[:, m * part:(m + 1) * part] for t in totals], axis=1)
    for c in range(CHUNKS):
        for j in range(1, cds):
            scatter(j, c).wait_send()


def solution(mesh):
    pairs, cds = mesh.shape["pair"], mesh.shape["cd"]
    nz = pairs // CORES

    def local(amplitudes, integrals, keep_tiles):
        n, depth = amplitudes.shape
        ab = integrals.shape[1]
        rows = n // cds
        return pl.pallas_call(
            functools.partial(kernel, pairs, cds),
            out_shape=pltpu.VMEM((rows, ab), jnp.float32),
            in_specs=[
                pl.BlockSpec(memory_space=pl.ANY),
                pl.BlockSpec(memory_space=pl.ANY),
                pl.BlockSpec(memory_space=pl.ANY),
            ],
            out_specs=pl.BlockSpec(memory_space=pltpu.VMEM),
            scratch_shapes=[
                pltpu.SMEM(keep_tiles.shape[::-1], jnp.int32),
                pltpu.VMEM(integrals.shape, jnp.float32),
                pltpu.VMEM((n, depth), jnp.float32),
                pltpu.VMEM((pairs, TILE, TILE), jnp.float32),
                pltpu.VMEM((n, depth), jnp.bfloat16),
                pltpu.VMEM((n, depth), jnp.bfloat16),
                pltpu.VMEM((CHUNKS, n, ab // CHUNKS), jnp.float32),
                pltpu.VMEM((cds - 1, CHUNKS, rows, ab // CHUNKS), jnp.float32),
                pltpu.SemaphoreType.DMA((3,)),
                pltpu.SemaphoreType.DMA((2, nz, CHUNKS)),
                pltpu.SemaphoreType.DMA((2, nz, CHUNKS)),
                pltpu.SemaphoreType.DMA((2, nz, CHUNKS)),
                pltpu.SemaphoreType.DMA((2, nz, CHUNKS)),
                pltpu.SemaphoreType.DMA((cds - 1, CHUNKS)),
                pltpu.SemaphoreType.DMA((cds - 1, CHUNKS)),
            ],
            compiler_params=pltpu.CompilerParams(collective_id=0, has_side_effects=True),
        )(keep_tiles.T, integrals, amplitudes)

    placed = (P("pair", "cd"), P(("cd", "pair"), None), P())
    return jax.shard_map(
        local, mesh=mesh, in_specs=placed, out_specs=P(("pair", "cd"), None), check_vma=False
    )
```

```python
import functools

import jax
import jax.numpy as jnp
from jax import lax
from jax.experimental import pallas as pl
from jax.experimental.pallas import tpu as pltpu
from jax.sharding import PartitionSpec as P

TILE = 128
CORES = 2
CHUNKS = 2
MESH = pl.DeviceIdType.MESH


def flip(i, bits):
    b = 1
    out = i
    while b <= bits:
        if bits & b:
            out = out + b - 2 * b * (lax.rem(lax.div(i, b), 2))
        b *= 2
    return out


def split(x):
    hi = x.astype(jnp.bfloat16)
    lo = (x - hi.astype(jnp.float32)).astype(jnp.bfloat16)
    return hi, lo


def dot3(a_hi, a_lo, b_hi, b_lo):
    d = functools.partial(
        lax.dot_general, dimension_numbers=(((1,), (1,)), ((), ())), preferred_element_type=jnp.float32)
    return d(a_hi, b_hi) + (d(a_lo, b_hi) + d(a_hi, b_lo))


def kernel(pairs, cds, flags_hbm, v_hbm, a_hbm, out_ref, flags, v, a, tiles, a_hi, a_lo, acc, land,
           load_sem, ssem, rsem, psend, precv, rs_send, rs_recv):
    nz = pairs // CORES
    me = lax.axis_index("pair")
    cd = lax.axis_index("cd")
    z = lax.div(me, CORES)
    core = lax.rem(me, CORES)
    partner = me + 1 - 2 * core
    blocks = v.shape[1] // TILE
    part = TILE // CHUNKS
    rows = out_ref.shape[0]

    def valid(d, s):
        return z - s >= 0 if d == 0 else z + s < nz

    load_v = pltpu.make_async_copy(v_hbm, v, load_sem.at[0])
    load_v.start()
    load_f = pltpu.make_async_copy(flags_hbm, flags, load_sem.at[2])
    load_f.start()
    load_a = pltpu.make_async_copy(a_hbm, a, load_sem.at[1])
    load_a.start()

    has_next = (z + 1 < nz, z > 0)
    neighbour = (me + CORES, me - CORES)

    barrier = pltpu.get_barrier_semaphore()
    for d in range(2):
        for s in range(nz - 1):
            far = me + (s + 1) * CORES if d == 0 else me - (s + 1) * CORES
            @pl.when(valid(1 - d, s + 1))
            def _():
                pl.semaphore_signal(barrier, inc=1, device_id={"pair": far}, device_id_type=MESH)
    for j in range(1, cds):
        pl.semaphore_signal(barrier, inc=1, device_id={"cd": flip(cd, j)}, device_id_type=MESH)
    pl.semaphore_signal(barrier, inc=1, device_id={"pair": partner}, device_id_type=MESH)

    load_f.wait()
    load_v.wait()
    row_block = cd * pairs + me
    own = v[:, :TILE] * flags[0, row_block].astype(jnp.float32)
    for m in range(1, blocks):
        own = own + v[:, m * TILE:(m + 1) * TILE] * flags[m, row_block].astype(jnp.float32)
    tiles[me] = own.T

    greeted = cds + nz - 1
    pl.semaphore_wait(barrier, greeted)

    def stream(d, s, c, k):
        r = pl.ds(c * part, part)
        far = me + (s + 1) * CORES if d == 0 else me - (s + 1) * CORES
        return pltpu.make_async_remote_copy(
            src_ref=tiles.at[k, r], dst_ref=tiles.at[k, r],
            send_sem=ssem.at[d, s, c], recv_sem=rsem.at[d, s, c],
            device_id={"pair": far}, device_id_type=MESH)

    def exchange(d, s, c, k):
        r = pl.ds(c * part, part)
        return pltpu.make_async_remote_copy(
            src_ref=tiles.at[k, r], dst_ref=tiles.at[k, r],
            send_sem=psend.at[d, s, c], recv_sem=precv.at[d, s, c],
            device_id={"pair": partner}, device_id_type=MESH)

    def origin(d, s):
        return z - s if d == 0 else z + s

    for c in range(CHUNKS):
        for s in range(nz - 2, -1, -1):
            for d in (1, 0):
                @pl.when(valid(1 - d, s + 1))
                def _():
                    stream(d, s, c, me).start()
    for c in range(CHUNKS):
        exchange(0, 0, c, me).start()

    load_a.wait()
    hi, lo = split(a[...])
    a_hi[...] = hi
    a_lo[...] = lo

    def compute(d, s, c):
        chip = origin(d, s)
        exchange(d, s, c, chip * CORES + 1 - core).wait_recv()
        halves = []
        for i in range(CORES):
            k = chip * CORES + i
            t = tiles[k, c * part:(c + 1) * part]
            g = cd * pairs + k
            halves.append(jnp.concatenate(
                [t * flags[m, g].astype(jnp.float32) for m in range(blocks)], axis=0))
        b_hi, b_lo = split(jnp.concatenate(halves, axis=1))
        cols = pl.ds(pl.multiple_of(chip * (CORES * TILE), CORES * TILE), CORES * TILE)
        prod = dot3(a_hi[:, cols], a_lo[:, cols], b_hi, b_lo)
        if s == 0:
            acc[c] = prod
        else:
            acc[c] += prod

    def compute_step(s, c):
        if s == 0:
            compute(0, 0, c)
        else:
            for d in range(2):
                @pl.when(valid(d, s))
                def _():
                    compute(d, s, c)

    for s in range(1, nz):
        for c in range(CHUNKS):
            for d in range(2):
                @pl.when(valid(d, s))
                def _():
                    k = origin(d, s) * CORES + core
                    stream(d, s - 1, c, k).wait_recv()
                    exchange(d, s, c, k).start()
            compute_step(s - 1, c)

    def scatter(j, c):
        q = flip(cd, j)
        return pltpu.make_async_remote_copy(
            src_ref=acc.at[c, pl.ds(pl.multiple_of(q * rows, rows), rows)], dst_ref=land.at[j - 1, c],
            send_sem=rs_send.at[j - 1, c], recv_sem=rs_recv.at[j - 1, c],
            device_id={"cd": q}, device_id_type=MESH)

    for c in range(CHUNKS):
        compute_step(nz - 1, c)
        for j in range(cds - 1, 0, -1):
            scatter(j, c).start()

    for c in range(CHUNKS):
        exchange(0, 0, c, me).wait_send()
        for d in range(2):
            for s in range(nz - 1):
                @pl.when(valid(1 - d, s + 1))
                def _():
                    stream(d, s, c, me).wait_send()
    for s in range(1, nz):
        for d in range(2):
            @pl.when(valid(d, s))
            def _():
                k = origin(d, s) * CORES + core
                for c in range(CHUNKS):
                    exchange(d, s, c, k).wait_send()

    totals = []
    for c in range(CHUNKS):
        total = acc[c, pl.ds(pl.multiple_of(cd * rows, rows), rows)]
        for j in range(1, cds):
            scatter(j, c).wait_recv()
            total = total + land[j - 1, c]
        totals.append(total)
    for m in range(blocks):
        out_ref[:, m * TILE:(m + 1) * TILE] = jnp.concatenate(
            [t[:, m * part:(m + 1) * part] for t in totals], axis=1)
    for c in range(CHUNKS):
        for j in range(1, cds):
            scatter(j, c).wait_send()


def solution(mesh):
    pairs, cds = mesh.shape["pair"], mesh.shape["cd"]
    nz = pairs // CORES

    def local(amplitudes, integrals, keep_tiles):
        n, depth = amplitudes.shape
        ab = integrals.shape[1]
        rows = n // cds
        return pl.pallas_call(
            functools.partial(kernel, pairs, cds),
            out_shape=pltpu.VMEM((rows, ab), jnp.float32),
            in_specs=[
                pl.BlockSpec(memory_space=pl.ANY),
                pl.BlockSpec(memory_space=pl.ANY),
                pl.BlockSpec(memory_space=pl.ANY),
            ],
            out_specs=pl.BlockSpec(memory_space=pltpu.VMEM),
            scratch_shapes=[
                pltpu.SMEM(keep_tiles.shape[::-1], jnp.int32),
                pltpu.VMEM(integrals.shape, jnp.float32),
                pltpu.VMEM((n, depth), jnp.float32),
                pltpu.VMEM((pairs, TILE, TILE), jnp.float32),
                pltpu.VMEM((n, depth), jnp.bfloat16),
                pltpu.VMEM((n, depth), jnp.bfloat16),
                pltpu.VMEM((CHUNKS, n, ab // CHUNKS), jnp.float32),
                pltpu.VMEM((cds - 1, CHUNKS, rows, ab // CHUNKS), jnp.float32),
                pltpu.SemaphoreType.DMA((3,)),
                pltpu.SemaphoreType.DMA((2, nz, CHUNKS)),
                pltpu.SemaphoreType.DMA((2, nz, CHUNKS)),
                pltpu.SemaphoreType.DMA((2, nz, CHUNKS)),
                pltpu.SemaphoreType.DMA((2, nz, CHUNKS)),
                pltpu.SemaphoreType.DMA((cds - 1, CHUNKS)),
                pltpu.SemaphoreType.DMA((cds - 1, CHUNKS)),
            ],
            compiler_params=pltpu.CompilerParams(collective_id=0, has_side_effects=True),
        )(keep_tiles.T, integrals, amplitudes)

    placed = (P("pair", "cd"), P(("cd", "pair"), None), P())
    return jax.shard_map(
        local, mesh=mesh, in_specs=placed, out_specs=P(("pair", "cd"), None), check_vma=False
    )
```

```python
import functools

import jax
import jax.numpy as jnp
from jax import lax
from jax.experimental import pallas as pl
from jax.experimental.pallas import tpu as pltpu
from jax.sharding import PartitionSpec as P

TILE = 128
CORES = 2
CHUNKS = 1
MESH = pl.DeviceIdType.MESH


def flip(i, bits):
    b = 1
    out = i
    while b <= bits:
        if bits & b:
            out = out + b - 2 * b * (lax.rem(lax.div(i, b), 2))
        b *= 2
    return out


def split(x):
    hi = x.astype(jnp.bfloat16)
    lo = (x - hi.astype(jnp.float32)).astype(jnp.bfloat16)
    return hi, lo


def dot3(a_hi, a_lo, b_hi, b_lo):
    d = functools.partial(
        lax.dot_general, dimension_numbers=(((1,), (1,)), ((), ())), preferred_element_type=jnp.float32)
    return d(a_hi, b_hi) + (d(a_lo, b_hi) + d(a_hi, b_lo))


def kernel(pairs, cds, flags_hbm, v_hbm, a_hbm, out_ref, flags, v, a, tiles, a_hi, a_lo, acc, land,
           load_sem, ssem, rsem, psend, precv, rs_send, rs_recv):
    nz = pairs // CORES
    me = lax.axis_index("pair")
    cd = lax.axis_index("cd")
    z = lax.div(me, CORES)
    core = lax.rem(me, CORES)
    partner = me + 1 - 2 * core
    blocks = v.shape[1] // TILE
    part = TILE // CHUNKS
    rows = out_ref.shape[0]

    def valid(d, s):
        return z - s >= 0 if d == 0 else z + s < nz

    load_v = pltpu.make_async_copy(v_hbm, v, load_sem.at[0])
    load_v.start()
    load_f = pltpu.make_async_copy(flags_hbm, flags, load_sem.at[2])
    load_f.start()
    load_a = pltpu.make_async_copy(a_hbm, a, load_sem.at[1])
    load_a.start()

    has_next = (z + 1 < nz, z > 0)
    neighbour = (me + CORES, me - CORES)

    barrier = pltpu.get_barrier_semaphore()
    for d in range(2):
        for s in range(nz - 1):
            far = me + (s + 1) * CORES if d == 0 else me - (s + 1) * CORES
            @pl.when(valid(1 - d, s + 1))
            def _():
                pl.semaphore_signal(barrier, inc=1, device_id={"pair": far}, device_id_type=MESH)
    for j in range(1, cds):
        pl.semaphore_signal(barrier, inc=1, device_id={"cd": flip(cd, j)}, device_id_type=MESH)
    pl.semaphore_signal(barrier, inc=1, device_id={"pair": partner}, device_id_type=MESH)

    load_f.wait()
    load_v.wait()
    row_block = cd * pairs + me
    own = v[:, :TILE] * flags[0, row_block].astype(jnp.float32)
    for m in range(1, blocks):
        own = own + v[:, m * TILE:(m + 1) * TILE] * flags[m, row_block].astype(jnp.float32)
    tiles[me] = own.T

    greeted = cds + nz - 1
    pl.semaphore_wait(barrier, greeted)

    def stream(d, s, c, k):
        r = pl.ds(c * part, part)
        far = me + (s + 1) * CORES if d == 0 else me - (s + 1) * CORES
        return pltpu.make_async_remote_copy(
            src_ref=tiles.at[k, r], dst_ref=tiles.at[k, r],
            send_sem=ssem.at[d, s, c], recv_sem=rsem.at[d, s, c],
            device_id={"pair": far}, device_id_type=MESH)

    def exchange(d, s, c, k):
        r = pl.ds(c * part, part)
        return pltpu.make_async_remote_copy(
            src_ref=tiles.at[k, r], dst_ref=tiles.at[k, r],
            send_sem=psend.at[d, s, c], recv_sem=precv.at[d, s, c],
            device_id={"pair": partner}, device_id_type=MESH)

    def origin(d, s):
        return z - s if d == 0 else z + s

    for s in range(nz - 2, -1, -1):
        for c in range(CHUNKS):
            for d in (1, 0):
                @pl.when(valid(1 - d, s + 1))
                def _():
                    stream(d, s, c, me).start()
    for c in range(CHUNKS):
        exchange(0, 0, c, me).start()

    load_a.wait()
    hi, lo = split(a[...])
    a_hi[...] = hi
    a_lo[...] = lo

    def compute(d, s, c):
        chip = origin(d, s)
        exchange(d, s, c, chip * CORES + 1 - core).wait_recv()
        halves = []
        for i in range(CORES):
            k = chip * CORES + i
            t = tiles[k, c * part:(c + 1) * part]
            g = cd * pairs + k
            halves.append(jnp.concatenate(
                [t * flags[m, g].astype(jnp.float32) for m in range(blocks)], axis=0))
        b_hi, b_lo = split(jnp.concatenate(halves, axis=1))
        cols = pl.ds(pl.multiple_of(chip * (CORES * TILE), CORES * TILE), CORES * TILE)
        prod = dot3(a_hi[:, cols], a_lo[:, cols], b_hi, b_lo)
        if s == 0:
            acc[c] = prod
        else:
            acc[c] += prod

    def compute_step(s, c):
        if s == 0:
            compute(0, 0, c)
        else:
            for d in range(2):
                @pl.when(valid(d, s))
                def _():
                    compute(d, s, c)

    for s in range(1, nz):
        for c in range(CHUNKS):
            for d in range(2):
                @pl.when(valid(d, s))
                def _():
                    k = origin(d, s) * CORES + core
                    stream(d, s - 1, c, k).wait_recv()
                    exchange(d, s, c, k).start()
            compute_step(s - 1, c)

    def scatter(j, c):
        q = flip(cd, j)
        return pltpu.make_async_remote_copy(
            src_ref=acc.at[c, pl.ds(pl.multiple_of(q * rows, rows), rows)], dst_ref=land.at[j - 1, c],
            send_sem=rs_send.at[j - 1, c], recv_sem=rs_recv.at[j - 1, c],
            device_id={"cd": q}, device_id_type=MESH)

    for c in range(CHUNKS):
        compute_step(nz - 1, c)
        for j in range(cds - 1, 0, -1):
            scatter(j, c).start()

    for c in range(CHUNKS):
        exchange(0, 0, c, me).wait_send()
        for d in range(2):
            for s in range(nz - 1):
                @pl.when(valid(1 - d, s + 1))
                def _():
                    stream(d, s, c, me).wait_send()
    for s in range(1, nz):
        for d in range(2):
            @pl.when(valid(d, s))
            def _():
                k = origin(d, s) * CORES + core
                for c in range(CHUNKS):
                    exchange(d, s, c, k).wait_send()

    totals = []
    for c in range(CHUNKS):
        total = acc[c, pl.ds(pl.multiple_of(cd * rows, rows), rows)]
        for j in range(1, cds):
            scatter(j, c).wait_recv()
            total = total + land[j - 1, c]
        totals.append(total)
    for m in range(blocks):
        out_ref[:, m * TILE:(m + 1) * TILE] = jnp.concatenate(
            [t[:, m * part:(m + 1) * part] for t in totals], axis=1)
    for c in range(CHUNKS):
        for j in range(1, cds):
            scatter(j, c).wait_send()


def solution(mesh):
    pairs, cds = mesh.shape["pair"], mesh.shape["cd"]
    nz = pairs // CORES

    def local(amplitudes, integrals, keep_tiles):
        n, depth = amplitudes.shape
        ab = integrals.shape[1]
        rows = n // cds
        return pl.pallas_call(
            functools.partial(kernel, pairs, cds),
            out_shape=pltpu.VMEM((rows, ab), jnp.float32),
            in_specs=[
                pl.BlockSpec(memory_space=pl.ANY),
                pl.BlockSpec(memory_space=pl.ANY),
                pl.BlockSpec(memory_space=pl.ANY),
            ],
            out_specs=pl.BlockSpec(memory_space=pltpu.VMEM),
            scratch_shapes=[
                pltpu.SMEM(keep_tiles.shape[::-1], jnp.int32),
                pltpu.VMEM(integrals.shape, jnp.float32),
                pltpu.VMEM((n, depth), jnp.float32),
                pltpu.VMEM((pairs, TILE, TILE), jnp.float32),
                pltpu.VMEM((n, depth), jnp.bfloat16),
                pltpu.VMEM((n, depth), jnp.bfloat16),
                pltpu.VMEM((CHUNKS, n, ab // CHUNKS), jnp.float32),
                pltpu.VMEM((cds - 1, CHUNKS, rows, ab // CHUNKS), jnp.float32),
                pltpu.SemaphoreType.DMA((3,)),
                pltpu.SemaphoreType.DMA((2, nz, CHUNKS)),
                pltpu.SemaphoreType.DMA((2, nz, CHUNKS)),
                pltpu.SemaphoreType.DMA((2, nz, CHUNKS)),
                pltpu.SemaphoreType.DMA((2, nz, CHUNKS)),
                pltpu.SemaphoreType.DMA((cds - 1, CHUNKS)),
                pltpu.SemaphoreType.DMA((cds - 1, CHUNKS)),
            ],
            compiler_params=pltpu.CompilerParams(collective_id=0, has_side_effects=True),
        )(keep_tiles.T, integrals, amplitudes)

    placed = (P("pair", "cd"), P(("cd", "pair"), None), P())
    return jax.shard_map(
        local, mesh=mesh, in_specs=placed, out_specs=P(("pair", "cd"), None), check_vma=False
    )
```
